256 devices in a mesh: dp: 32 (over x, z_lo, core), expert: 8 (over y, z_hi).
Axes of the slice: x: 4, y: 4, z: 8 (z_hi: 2, z_lo: 4; z = z_hi * 4 + z_lo), core: 2. Of those that a mesh axis runs over, the one named last changes fastest.
Arguments:
- grad_out: bfloat16 [131072, 3072], P(('dp', 'expert')), may hold values from -0.19921875 to 0.19921875
- expert_ids: int32 [131072, 2], P(('dp', 'expert')), may hold values from 0 to 7, all different within a row; in each aligned block of 512 rows (0 to 511, 512 to 1023, ...) at most 192 rows name the same one
- gate_probs: float32 [131072, 2], P(('dp', 'expert')), may hold values from 0.1 to 1
- saved_gate: bfloat16 [49152, 8, 1024], P('dp', 'expert'), may hold values from -6 to 6
- saved_up: bfloat16 [49152, 8, 1024], P('dp', 'expert'), may hold values from -6 to 6
- master: float32 [8, 1024, 3072], P('expert', 'dp')
- moment_one: float32 [8, 1024, 3072], P('expert', 'dp'), may hold values from -2 to 2
- moment_two: float32 [8, 1024, 3072], P('expert', 'dp'), may hold values from 0.05 to 1
Outputs:
- new_master: float32 [8, 1024, 3072], P('expert', 'dp')
- new_moment_one: float32 [8, 1024, 3072], P('expert', 'dp')
- new_moment_two: float32 [8, 1024, 3072], P('expert', 'dp')
- new_weights: float32 [8, 1024, 3072], P('expert')
The draws below stay inside these ranges and needn't reach their ends.
Inputs may be any that keep to these rules, and one draw needn't show every extreme that they name: `expert_ids`: in each aligned block of 512 rows (the tokens of one device) no expert is named by more than 192 rows, a bound that some block reaches.
All inputs are finite; a program needn't handle non-finite values.
Results may differ from the reference program's by a relative error of at most 0.00035.
Values may be sent and summed in bfloat16 or wider, within the bound.
A program may use at most 128 MiB of HBM per device.

```python
import math
import jax
import jax.numpy as jnp
import numpy as np
from jax import lax

D = 3072
EXPERTS_ALL = 8
HID_DEV = 1024
TOK_DEV = 512
BLOCKS = 8
CAP = 192
TOKENS = 131072
SLOTS = 49152


def draw_master(key, part):
    key_rows, key_cols, key_base = jax.random.split(key, 3)
    rows = jnp.exp(jax.random.uniform(key_rows, (BLOCKS, HID_DEV, 1), jnp.float32) * math.log(10.0))
    cols = jnp.exp(jax.random.uniform(key_cols, (1, 1, D), jnp.float32) * math.log(10.0))
    base = jax.random.normal(key_base, (BLOCKS, HID_DEV, D), jnp.float32)
    return (0.02 * rows * cols * base).astype(jnp.float32)


def block_levels(key, shape, pieces, low, top_value):
    def one(dim, parts):
        steps = jax.random.uniform(jax.random.fold_in(jax.random.fold_in(key, 6), dim), (parts,), jnp.float32, low / len(pieces), top_value / len(pieces))
        return jnp.repeat(jnp.exp(steps), shape[dim] // parts).reshape((-1,) + (1,) * (len(shape) - dim - 1))

    level = one(*pieces[0])
    for cut in pieces[1:]:
        level = level * one(*cut)
    return level


def routed_block(stream_key, own, number, rows, amount, top, limit, skew):
    order = jax.random.permutation(stream_key, amount)
    packed, usual = load_shares(amount, rows * top, limit, skew, True), load_shares(amount, rows * top, limit, skew, False)
    places = jnp.arange(amount)

    def named(tallies, turn):
        used = int((tallies > 0).sum())
        fixed = max(1, used // 4)
        passed = fixed + (places - fixed + turn * (used - fixed)) % max(1, amount - fixed)
        return jnp.zeros((amount,), jnp.int32).at[order[jnp.where(places < fixed, places, passed)]].set(jnp.asarray(tallies, jnp.int32))

    tallies = jnp.where(number % 4 == 0, named(packed, number // 4), named(usual, number - number // 4 - 1))
    mixed = jax.random.permutation(jax.random.fold_in(own, 3), amount)
    giver, sink = mixed[0:amount // 2 * 2:2], mixed[1:amount // 2 * 2:2]
    slack = jnp.minimum(tallies[giver] - 1, limit - tallies[sink]) // 2
    slack = jnp.where((giver == order[0]) | (sink == order[0]) | (tallies[sink] == 0), 0, jnp.maximum(slack, 0))
    passed = jax.random.randint(jax.random.fold_in(own, 4), (amount // 2,), 0, 1 << 20) % (slack + 1)
    tallies = tallies.at[giver].add(-passed).at[sink].add(passed)
    members = jnp.searchsorted(jnp.cumsum(tallies), jnp.arange(rows * top), side="right").astype(jnp.int32)
    grid = members.reshape(top, rows).T
    grid = grid[jax.random.permutation(jax.random.fold_in(own, 1), rows)]
    turn = jax.random.randint(jax.random.fold_in(own, 2), (rows, 1), 0, top)
    return jnp.take_along_axis(grid, (jnp.arange(top)[None, :] + turn) % top, axis=1)


def load_shares(count, total, limit, slope, full):
    loads = [(1 << 20) // math.isqrt(grade ** slope) + 1 for grade in range(1, count + 1)]
    largest = limit if full else min(limit, max(-(-total // count), total * loads[0] // sum(loads)))
    least = 1 if total - largest >= count - 1 else 0
    holding, rest = [largest] + [least] * (count - 1), total - largest - least * (count - 1)
    while rest > 0:
        candidates = [i for i in range(1, count) if holding[i] < largest] or [i for i in range(1, count) if holding[i] < limit]
        whole, budget = sum([loads[i] for i in candidates]), rest
        for i in candidates:
            extra = min(limit - holding[i], max(1, budget * loads[i] // whole), rest)
            holding[i] = holding[i] + extra
            rest = rest - extra
    return np.array(holding)


def centred(key, extent, scale, most, shards=(), kind=jnp.bfloat16):
    drawn = scale * jax.random.normal(key, extent, jnp.float32)
    if shards:
        drawn = drawn * block_levels(key, extent, shards, -0.22, 0.18)
    return jnp.clip(drawn, -most, most).astype(kind)


def setup_inputs(seed: int = 0) -> dict:
    key_list = jax.random.split(jax.random.key(seed), 9)
    grad_out = centred(key_list[0], (TOKENS, D), 0.03, 0.19921875, ((0, 256),))
    expert_ids_keys = jax.random.split(jax.random.fold_in(key_list[1], 1), TOKENS // TOK_DEV)
    expert_ids_turns = jax.random.permutation(jax.random.fold_in(key_list[1], 3), TOKENS // TOK_DEV)
    expert_ids = jax.vmap(lambda own, number: routed_block(jax.random.fold_in(key_list[1], 2), own, number, TOK_DEV, EXPERTS_ALL, 2, CAP, 2))(expert_ids_keys, expert_ids_turns).reshape((TOKENS, 2))
    gate_probs = jnp.clip(0.1 + 0.9 * jax.random.uniform(key_list[2], (TOKENS, 2), jnp.float32) ** block_levels(key_list[2], (TOKENS, 2), ((0, 256),), -0.2, 0.2), 0.1, 1.0)
    saved_gate = centred(key_list[3], (SLOTS, BLOCKS, HID_DEV), 1.0, 6.0, ((0, 32), (1, 8)))
    saved_up = centred(key_list[4], (SLOTS, BLOCKS, HID_DEV), 1.0, 6.0, ((0, 32), (1, 8)))
    master = draw_master(jax.random.fold_in(key_list[8], 71), 0)
    moment_one = centred(key_list[6], (BLOCKS, HID_DEV, D), 0.3, 2.0, ((0, 8), (1, 32)), jnp.float32)
    moment_two = jnp.clip(jnp.exp(math.log(1.0) - 2.9957323 * jax.random.uniform(key_list[7], (BLOCKS, HID_DEV, D), jnp.float32) ** block_levels(key_list[7], (BLOCKS, HID_DEV, D), ((0, 8), (1, 32)), -0.2, 0.2)), 0.05, 1.0)
    return dict(grad_out=grad_out, expert_ids=expert_ids, gate_probs=gate_probs, saved_gate=saved_gate, saved_up=saved_up, master=master, moment_one=moment_one, moment_two=moment_two)


def block_grad(pair, dispatched):
    gate_part, up_part = pair
    hidden = (jax.nn.silu(gate_part.astype(jnp.float32)) * up_part.astype(jnp.float32)).astype(jnp.bfloat16)
    return jnp.dot(hidden.T, dispatched, preferred_element_type=jnp.float32)

def reference(grad_out, expert_ids, gate_probs, saved_gate, saved_up, master, moment_one, moment_two):
    groups = TOKENS // TOK_DEV
    ids = expert_ids.reshape(groups, TOK_DEV, 2)
    probs = gate_probs.reshape(groups, TOK_DEV, 2)
    hit = ids == 0
    chosen = jnp.any(hit, axis=2)
    weight = lax.optimization_barrier(jnp.sum(jnp.where(hit, probs, jnp.float32(0.0)), axis=2))
    slot = jnp.cumsum(chosen.astype(jnp.int32), axis=1).astype(jnp.int32) - 1
    scaled = (weight[:, :, None] * grad_out.reshape(groups, TOK_DEV, D).astype(jnp.float32)).astype(jnp.bfloat16)
    places = jnp.arange(CAP, dtype=jnp.int32)
    placing = ((slot[:, None, :] == places[None, :, None]) & chosen[:, None, :]).astype(jnp.float32)
    dispatched = jnp.einsum('bct,btd->bcd', placing, scaled.astype(jnp.float32)).astype(jnp.bfloat16)
    dispatched = dispatched.reshape(groups * CAP, D)
    gates = jnp.moveaxis(saved_gate, 1, 0)
    ups = jnp.moveaxis(saved_up, 1, 0)
    grad = lax.map(lambda pair: block_grad(pair, dispatched), (gates, ups))
    new_one = 0.9 * moment_one + 0.1 * grad
    new_two = 0.95 * moment_two + 0.05 * grad * grad
    step = new_one / (1.0 - 0.9 ** 20) / (jnp.sqrt(new_two / (1.0 - 0.95 ** 20)) + 1e-08)
    wrms = jnp.sqrt(lax.optimization_barrier(jnp.mean(master * master, axis=-1, keepdims=True)) + 1e-06)
    srms = jnp.sqrt(lax.optimization_barrier(jnp.mean(step * step, axis=-1, keepdims=True)) + 1e-06)
    factor = jnp.minimum(1.0, 0.02 * wrms / (0.01 * srms))
    new_master = master - 0.01 * factor * step
    return (new_master, new_one, new_two, new_master)
```

```python
import functools

import jax
import jax.numpy as jnp
from jax import lax
from jax.experimental import pallas as pl
from jax.experimental.pallas import tpu as pltpu
from jax.sharding import PartitionSpec as P

MESH = pl.DeviceIdType.MESH
NX, NZ, NC, NY, NH = 4, 4, 2, 4, 2
CHUNKS = 6
AHEAD = 2
LEVELS = 32766.0
LOG2E = 1.4426950408889634
LN2 = 0.6931471805599453


def exponent(top):
    return jnp.floor(jnp.log(jnp.maximum(top, 1e-30)) * LOG2E) + 1.0


def code(x, e):
    return jnp.floor(x * (jnp.exp(e * -LN2) * LEVELS) + 0.5).astype(jnp.int32).astype(jnp.int16)


def scale_of(e16):
    return jnp.exp(e16.astype(jnp.int32).astype(jnp.float32) * LN2) * (1.0 / LEVELS)


def value(q, scale):
    return q.astype(jnp.int32).astype(jnp.float32) * scale


def encode_rows(src, start, rows, dst):
    tile = 32
    width = dst.shape[-1]

    def top(i, m):
        at = pl.multiple_of(start + i * tile, tile)
        return jnp.maximum(m, jnp.abs(src[pl.ds(at, tile), :]))

    m = lax.fori_loop(0, rows // tile, top, jnp.zeros((tile, width), jnp.float32))
    e = exponent(jnp.max(m, axis=0, keepdims=True))

    def put(i, carry):
        at = pl.multiple_of(start + i * tile, tile)
        to = pl.multiple_of(i * tile, tile)
        dst[pl.ds(to, tile), :] = code(src[pl.ds(at, tile), :], e)
        return carry

    lax.fori_loop(0, rows // tile, put, 0)
    dst[pl.ds(rows, 16), :] = jnp.broadcast_to(e, (16, width)).astype(jnp.int32).astype(jnp.int16)


def kernel(ids, probs, gout, gate, up, mas, mo1, mo2, nm_o, m1_o, m2_o, q_o,
           go_v, gate_v, up_v, mas_v, m1_v, m2_v, place, wslot, H, G, acc, pacc, xacc, step_v, ssum,
           csend, crecv, xsend, xrecv, zsend, zrecv, own_q,
           lsem, ssem, rsem, gs, gr):
    dp = lax.axis_index("dp")
    ex = lax.axis_index("expert")
    core, zl, x = dp % NC, (dp // NC) % NZ, dp // (NC * NZ)
    y, zh = ex // NH, ex % NH
    cap = place.shape[0]
    half = cap // 2
    C, _, dc = go_v.shape
    own_rows, D = mas_v.shape

    def at(x_, z_, c_, y_, h_):
        return ((x_ * NZ + z_) * NC + c_, y_ * NH + h_)

    ym, yp = (y + NY - 1) % NY, (y + 1) % NY
    yo = (y + 2) % NY
    dev_z = at(x, zl, core, y, 1 - zh)
    dev_yp, dev_ym = at(x, zl, core, yp, zh), at(x, zl, core, ym, zh)
    dev_c = at(x, zl, 1 - core, y, zh)
    dev_x = [at((x + k) % NX, zl, core, y, zh) for k in range(1, NX)]
    dev_zl = [at(x, (zl + k) % NZ, core, y, zh) for k in range(1, NZ)]
    peers = [dev_z, dev_yp, dev_ym, dev_c] + dev_x + dev_zl

    def local(i):
        if i < C:
            return pltpu.make_async_copy(gout.at[:, pl.ds(i * dc, dc)], go_v.at[i], lsem.at[i])
        src, dst = ((gate, gate_v), (up, up_v), (mas, mas_v), (mo1, m1_v), (mo2, m2_v))[i - C]
        return pltpu.make_async_copy(src, dst, lsem.at[i])

    for i in range(C + 5):
        local(i).start()

    barrier = pltpu.get_barrier_semaphore()
    for dev in peers:
        pl.semaphore_signal(barrier, inc=1, device_id=dev, device_id_type=MESH)

    tokens = ids.shape[1]
    hit0, hit1 = ids[0:1, :] == 0, ids[1:2, :] == 0
    chosen = jnp.where(hit0 | hit1, 1.0, 0.0)
    weight = jnp.where(hit0, probs[0:1, :], 0.0) + jnp.where(hit1, probs[1:2, :], 0.0)
    before = lax.broadcasted_iota(jnp.int32, (tokens, tokens), 0) < lax.broadcasted_iota(jnp.int32, (tokens, tokens), 1)
    count = jnp.dot(
        jnp.broadcast_to(chosen, (16, tokens)).astype(jnp.bfloat16),
        jnp.where(before, 1.0, 0.0).astype(jnp.bfloat16),
        preferred_element_type=jnp.float32,
    )
    slot = jnp.where(chosen > 0.5, count[0:1, :], -1.0)
    mark = lax.broadcasted_iota(jnp.int32, (cap, tokens), 0).astype(jnp.float32) == slot
    place[...] = jnp.where(mark, 1.0, 0.0).astype(jnp.bfloat16)
    wslot[...] = jnp.broadcast_to(jnp.sum(jnp.where(mark, weight, 0.0), axis=1, keepdims=True), wslot.shape)

    def block(c, y_, h_, lo=0, rows=None):
        e = y_ * NH + h_
        return G.at[c, pl.ds(pl.multiple_of(e * cap + lo, 32), cap if rows is None else rows), :]

    def copy(kind, c, src, dst, dev):
        return pltpu.make_async_remote_copy(
            src_ref=src, dst_ref=dst, send_sem=ssem.at[kind, c], recv_sem=rsem.at[kind, c],
            device_id=dev, device_id_type=MESH)

    def gather_copy(kind, c):
        if kind == 0:
            b, dev = block(c, y, zh), dev_z
        elif kind in (1, 2):
            b, dev = block(c, y, zh), (dev_yp if kind == 1 else dev_ym)
        elif kind in (3, 7):
            b, dev = block(c, ym, zh if kind == 3 else 1 - zh, 0, half), dev_yp
        elif kind in (4, 8):
            b, dev = block(c, yp, zh if kind == 4 else 1 - zh, half, half), dev_ym
        else:
            b, dev = block(c, y, 1 - zh), (dev_yp if kind == 5 else dev_ym)
        return copy(kind, c, b, b, dev)

    def gather_arrival(kind, c):
        if kind == 0:
            b = block(c, y, 1 - zh)
        elif kind in (1, 5):
            b = block(c, ym, zh if kind == 1 else 1 - zh)
        elif kind in (2, 6):
            b = block(c, yp, zh if kind == 2 else 1 - zh)
        elif kind in (3, 7):
            b = block(c, yo, zh if kind == 3 else 1 - zh, 0, half)
        else:
            b = block(c, yo, zh if kind == 4 else 1 - zh, half, half)
        return copy(kind, c, b, b, dev_z)

    def core_copy(c):
        return copy(9, c, csend.at[c], crecv.at[c], dev_c)

    def x_copy(c, k):
        return copy(9 + k, c, xsend.at[c, k - 1], xrecv.at[c, k - 1], dev_x[k - 1])

    def z_copy(c, k):
        return copy(12 + k, c, zsend.at[c, k - 1], zrecv.at[c, k - 1], dev_zl[k - 1])

    def fill(c):
        pltpu.make_async_copy(gout.at[:, pl.ds(0, dc)], go_v.at[c], lsem.at[c]).wait()
        rows = jnp.dot(place[...], go_v[c], preferred_element_type=jnp.float32)
        block(c, y, zh)[...] = (rows * wslot[:, 0:1]).astype(jnp.bfloat16)
        for kind in (0, 1, 2):
            gather_copy(kind, c).start()

    fill_first = min(AHEAD, C)
    pl.semaphore_wait(barrier, len(peers))
    for c in range(fill_first):
        fill(c)

    local(C).wait()
    local(C + 1).wait()

    def make_hidden(b, carry):
        cols = pl.ds(pl.multiple_of(b * 128, 128), 128)
        g = gate_v[:, cols].astype(jnp.float32)
        u = up_v[:, cols].astype(jnp.float32)
        h = (g / (1.0 + jnp.exp(-g)) * u).astype(jnp.bfloat16).T
        to = pl.multiple_of(b * 64, 64)
        H[0, pl.ds(to, 32), :] = h[0:32]
        H[1, pl.ds(to, 32), :] = h[32:64]
        H[0, pl.ds(to + 32, 32), :] = h[64:96]
        H[1, pl.ds(to + 32, 32), :] = h[96:128]
        return carry

    lax.fori_loop(0, gate_v.shape[1] // 128, make_hidden, 0)
    for i in range(2, 5):
        local(C + i).wait()
    ssum[...] = jnp.zeros_like(ssum)

    hrows = H.shape[1]
    xrows = hrows // NX
    zrows = xrows // NZ

    def stage_b(c):
        for kind in (1, 2):
            gather_arrival(kind, c).wait_recv()
            gather_copy(kind + 2, c).start()
        gather_arrival(0, c).wait_recv()
        for kind in (5, 6):
            gather_copy(kind, c).start()

    def stage_c(c):
        for kind in (5, 6):
            gather_arrival(kind, c).wait_recv()
            gather_copy(kind + 2, c).start()

    def stage_d(c):
        for kind in (3, 4, 7, 8):
            gather_arrival(kind, c).wait_recv()
        pacc[...] = jnp.dot(H[1 - core], G[c], preferred_element_type=jnp.float32)
        encode_rows(pacc, 0, hrows, csend.at[c])
        core_copy(c).start()
        acc[...] = jnp.dot(H[core], G[c], preferred_element_type=jnp.float32)
        core_copy(c).wait_recv()
        s = scale_of(crecv[c, pl.ds(hrows, 16), :])[0:1]

        def join(i, carry):
            rows = pl.ds(pl.multiple_of(i * 32, 32), 32)
            acc[rows, :] = acc[rows, :] + value(crecv[c, rows, :], s)
            return carry

        lax.fori_loop(0, hrows // 32, join, 0)
        for k in range(1, NX):
            encode_rows(acc, ((x + k) % NX) * xrows, xrows, xsend.at[c, k - 1])
            x_copy(c, k).start()

    def stage_e(c):
        scales = []
        for k in range(1, NX):
            x_copy(c, k).wait_recv()
            scales.append(scale_of(xrecv[c, k - 1, pl.ds(xrows, 16), :])[0:1])

        def join(i, carry):
            rows = pl.ds(pl.multiple_of(i * 32, 32), 32)
            total = acc[pl.ds(pl.multiple_of(x * xrows + i * 32, 32), 32), :]
            for k in range(1, NX):
                total = total + value(xrecv[c, k - 1, rows, :], scales[k - 1])
            xacc[rows, :] = total
            return carry

        lax.fori_loop(0, xrows // 32, join, 0)
        for k in range(1, NZ):
            encode_rows(xacc, ((zl + k) % NZ) * zrows, zrows, zsend.at[c, k - 1])
            z_copy(c, k).start()

    def stage_f(c):
        g = xacc[pl.ds(pl.multiple_of(zl * zrows, zrows), zrows), :]
        for k in range(1, NZ):
            z_copy(c, k).wait_recv()
            s = scale_of(zrecv[c, k - 1, pl.ds(zrows, 16), :])[0:1]
            g = g + value(zrecv[c, k - 1, pl.ds(0, zrows), :], s)
        cols = pl.ds(pl.multiple_of(c * dc, 128), dc)
        one = 0.9 * m1_v[:, cols] + 0.1 * g
        two = 0.95 * m2_v[:, cols] + 0.05 * g * g
        m1_o[:, cols] = one
        m2_o[:, cols] = two
        step = one / (1.0 - 0.9**20) / (jnp.sqrt(two / (1.0 - 0.95**20)) + 1e-08)
        step_v[:, cols] = step
        sq = step * step
        part = sq[:, 0:128]
        for j in range(1, dc // 128):
            part = part + sq[:, j * 128:(j + 1) * 128]
        ssum[...] += part

    def tick(t, carry):
        def guarded(stage, c):
            @pl.when((c >= 0) & (c < C))
            def _():
                stage(c)

        @pl.when(t + AHEAD < C)
        def _():
            fill(t + AHEAD)

        guarded(stage_b, t)
        guarded(stage_c, t - 1)
        guarded(stage_f, t - 4)
        guarded(stage_e, t - 3)
        guarded(stage_d, t - 2)
        return carry

    lax.fori_loop(0, C + 4, tick, 0)

    mas2 = mas_v[...] * mas_v[...]
    wrms = jnp.sqrt(jnp.sum(mas2, axis=1, keepdims=True) / D + 1e-06)
    srms = jnp.sqrt(jnp.sum(ssum[...], axis=1, keepdims=True) / D + 1e-06)
    factor = jnp.minimum(1.0, 0.02 * wrms / (0.01 * srms))
    new = mas_v[...] - 0.01 * factor * step_v[...]
    nm_o[...] = new
    top = jnp.abs(new[:, 0:128])
    for j in range(1, D // 128):
        top = jnp.maximum(top, jnp.abs(new[:, j * 128:(j + 1) * 128]))
    e = exponent(top)
    for j in range(D // 128):
        own_q[:, j * 128:(j + 1) * 128] = code(new[:, j * 128:(j + 1) * 128], e)
    own_q[:, D:D + 128] = e.astype(jnp.int32).astype(jnp.int16)

    def send(i, src, origin, dev):
        return pltpu.make_async_remote_copy(
            src_ref=src, dst_ref=q_o.at[origin], send_sem=gs.at[i], recv_sem=gr.at[i],
            device_id=dev, device_id_type=MESH)

    def home(x_, z_, c_):
        return (x_ * NZ + z_) * NC + c_

    def origin_z(k):
        return home(x, (zl + NZ - k) % NZ, core)

    sent = []

    def go(i, src, origin, dev):
        cp = send(i, src, origin, dev)
        cp.start()
        sent.append(cp)

    keep = pltpu.make_async_copy(own_q, q_o.at[dp], lsem.at[0])
    keep.start()
    for j in range(1, NX):
        go(3 + (j - 1) * 4, own_q, dp, dev_x[j - 1])
    for k in (1, 3, 2):
        go(k - 1, own_q, dp, dev_zl[k - 1])
    go(15, own_q, dp, dev_c)
    for k in (1, 3, 2):
        o = origin_z(k)
        send(k - 1, own_q, o, dev_c).wait_recv()
        for j in range(1, NX):
            go(3 + (j - 1) * 4 + k, q_o.at[o], o, dev_x[j - 1])
        go(15 + k, q_o.at[o], o, dev_c)
    for k in (0, 1, 3, 2):
        for j in (1, 3, 2):
            o = home((x + NX - j) % NX, (zl + NZ - k) % NZ, core)
            send(3 + (j - 1) * 4 + k, own_q, o, dev_c).wait_recv()
            go(15 + j * 4 + k, q_o.at[o], o, dev_c)
    for j in range(NX):
        for k in range(NZ):
            o = home((x + NX - j) % NX, (zl + NZ - k) % NZ, 1 - core)
            send(15 + j * 4 + k, own_q, o, dev_c).wait_recv()
    for cp in sent:
        cp.wait_send()
    keep.wait()

    def drain(c, carry):
        for kind in range(9):
            gather_copy(kind, c).wait_send()
        core_copy(c).wait_send()
        for k in range(1, NX):
            x_copy(c, k).wait_send()
        for k in range(1, NZ):
            z_copy(c, k).wait_send()
        return carry

    lax.fori_loop(0, C, drain, 0)


def decode(q_ref, a_ref, b_ref, c_ref, o_ref, a_o, b_o, c_o):
    blocks, rows, width = q_ref.shape

    @pl.when(pl.program_id(0) == 0)
    def _():
        a_o[...] = a_ref[...]
        b_o[...] = b_ref[...]
        c_o[...] = c_ref[...]

    for b in range(blocks):
        s = scale_of(q_ref[b, :, width - 128:])
        for j in range((width - 128) // 128):
            cols = slice(j * 128, (j + 1) * 128)
            o_ref[pl.ds(b * rows, rows), cols] = value(q_ref[b, :, cols], s)


def local(grad_out, expert_ids, gate_probs, saved_gate, saved_up, master, moment_one, moment_two):
    tokens, D = grad_out.shape
    cap = tokens * 3 // 8
    slots, _, width = saved_gate.shape
    rows = master.shape[1]
    devices = NX * NZ * NC
    C, dc = CHUNKS, D // CHUNKS
    f32, bf16, i16 = jnp.float32, jnp.bfloat16, jnp.int16
    vm = pl.BlockSpec(memory_space=pltpu.VMEM)
    hbm = pl.BlockSpec(memory_space=pl.ANY)
    hrows = width // NC
    xrows = hrows // NX
    outs = pl.pallas_call(
        kernel,
        name="step",
        out_shape=(
            jax.ShapeDtypeStruct((rows, D), f32),
            jax.ShapeDtypeStruct((rows, D), f32),
            jax.ShapeDtypeStruct((rows, D), f32),
            jax.ShapeDtypeStruct((devices, rows, D + 128), i16),
        ),
        in_specs=[vm, vm] + [hbm] * 6,
        out_specs=(vm, vm, vm, hbm),
        scratch_shapes=[
            pltpu.VMEM((C, tokens, dc), bf16),
            pltpu.VMEM((slots, width), bf16),
            pltpu.VMEM((slots, width), bf16),
            pltpu.VMEM((rows, D), f32),
            pltpu.VMEM((rows, D), f32),
            pltpu.VMEM((rows, D), f32),
            pltpu.VMEM((cap, tokens), bf16),
            pltpu.VMEM((cap, 128), f32),
            pltpu.VMEM((NC, hrows, slots), bf16),
            pltpu.VMEM((C, slots, dc), bf16),
            pltpu.VMEM((hrows, dc), f32),
            pltpu.VMEM((hrows, dc), f32),
            pltpu.VMEM((xrows, dc), f32),
            pltpu.VMEM((rows, D), f32),
            pltpu.VMEM((rows, 128), f32),
            pltpu.VMEM((C, hrows + 16, dc), i16),
            pltpu.VMEM((C, hrows + 16, dc), i16),
            pltpu.VMEM((C, NX - 1, xrows + 16, dc), i16),
            pltpu.VMEM((C, NX - 1, xrows + 16, dc), i16),
            pltpu.VMEM((C, NZ - 1, rows + 16, dc), i16),
            pltpu.VMEM((C, NZ - 1, rows + 16, dc), i16),
            pltpu.VMEM((rows, D + 128), i16),
            pltpu.SemaphoreType.DMA((C + 5,)),
            pltpu.SemaphoreType.DMA((16, C)),
            pltpu.SemaphoreType.DMA((16, C)),
            pltpu.SemaphoreType.DMA((31,)),
            pltpu.SemaphoreType.DMA((31,)),
        ],
        compiler_params=pltpu.CompilerParams(
            collective_id=0, has_side_effects=True, vmem_limit_bytes=60 << 20),
    )(
        expert_ids.T, gate_probs.T, grad_out,
        saved_gate.reshape(slots, width), saved_up.reshape(slots, width),
        master.reshape(rows, D), moment_one.reshape(rows, D), moment_two.reshape(rows, D),
    )
    new, one, two, q = outs
    per = 2
    whole = pl.BlockSpec((rows, D), lambda i: (0, 0))
    full, new, one, two = pl.pallas_call(
        decode,
        name="decode",
        grid=(devices // per,),
        out_shape=(jax.ShapeDtypeStruct((devices * rows, D), f32),) + (jax.ShapeDtypeStruct((rows, D), f32),) * 3,
        in_specs=[pl.BlockSpec((per, rows, D + 128), lambda i: (i, 0, 0)), whole, whole, whole],
        out_specs=(pl.BlockSpec((per * rows, D), lambda i: (i, 0)), whole, whole, whole),
    )(q, new, one, two)
    shape = master.shape
    return (new.reshape(shape), one.reshape(shape), two.reshape(shape), full.reshape(1, devices * rows, D))


def solution(mesh):
    return jax.shard_map(
        local,
        mesh=mesh,
        in_specs=(
            P(("dp", "expert"), None),
            P(("dp", "expert"), None),
            P(("dp", "expert"), None),
            P("dp", "expert", None),
            P("dp", "expert", None),
            P("expert", "dp", None),
            P("expert", "dp", None),
            P("expert", "dp", None),
        ),
        out_specs=(
            P("expert", "dp", None),
            P("expert", "dp", None),
            P("expert", "dp", None),
            P("expert", None, None),
        ),
        check_vma=False,
    )
```

```python
import functools

import jax
import jax.numpy as jnp
from jax import lax
from jax.experimental import pallas as pl
from jax.experimental.pallas import tpu as pltpu
from jax.sharding import PartitionSpec as P

MESH = pl.DeviceIdType.MESH
NX, NZ, NC, NY, NH = 4, 4, 2, 4, 2
CHUNKS = 8
AHEAD = 3
TILE = 32
LAG_E, LAG_F = 4, 6
LEVELS = 32766.0
LOG2E = 1.4426950408889634
LN2 = 0.6931471805599453


def exponent(top):
    return jnp.floor(jnp.log(jnp.maximum(top, 1e-30)) * LOG2E) + 1.0


def encode(x, dst, rows):
    n = x.shape[-1] // 128
    parts = [x[:, j * 128:(j + 1) * 128] for j in range(n)]
    top = jnp.abs(parts[0])
    for p in parts[1:]:
        top = jnp.maximum(top, jnp.abs(p))
    e = exponent(top)
    s = jnp.exp(e * -LN2) * LEVELS
    for j, p in enumerate(parts):
        dst[rows, j * 128:(j + 1) * 128] = jnp.floor(p * s + 0.5).astype(jnp.int32).astype(jnp.int16)
    dst[rows, n * 128:] = e.astype(jnp.int32).astype(jnp.int16)


def decoded(src, rows):
    n = src.shape[-1] // 128 - 1
    s = jnp.exp(src[rows, n * 128:].astype(jnp.int32).astype(jnp.float32) * LN2) * (1.0 / LEVELS)
    return [src[rows, j * 128:(j + 1) * 128].astype(jnp.int32).astype(jnp.float32) * s for j in range(n)]


def kernel(ids, probs, gout, gate, up, mas, mo1, mo2, nm_o, m1_o, m2_o, q_o,
           go_v, gate_v, up_v, mas_v, m1_v, m2_v, place, wslot, H, G, acc, xacc, step_v, ssum,
           csend, crecv, xsend, xrecv, zsend, zrecv, own_q,
           lsem, ssem, rsem, gs, gr):
    dp = lax.axis_index("dp")
    ex = lax.axis_index("expert")
    core, zl, x = dp % NC, (dp // NC) % NZ, dp // (NC * NZ)
    y, zh = ex // NH, ex % NH
    cap = place.shape[0]
    half = cap // 2
    C, _, dc = go_v.shape
    own_rows, D = mas_v.shape

    def at(x_, z_, c_, y_, h_):
        return ((x_ * NZ + z_) * NC + c_, y_ * NH + h_)

    ym, yp = (y + NY - 1) % NY, (y + 1) % NY
    yo = (y + 2) % NY
    dev_z = at(x, zl, core, y, 1 - zh)
    dev_yp, dev_ym = at(x, zl, core, yp, zh), at(x, zl, core, ym, zh)
    dev_c = at(x, zl, 1 - core, y, zh)
    dev_x = [at((x + k) % NX, zl, core, y, zh) for k in range(1, NX)]
    dev_zl = [at(x, (zl + k) % NZ, core, y, zh) for k in range(1, NZ)]
    peers = [dev_z, dev_yp, dev_ym, dev_c] + dev_x + dev_zl

    def local(i):
        if i < C:
            return pltpu.make_async_copy(gout.at[:, pl.ds(i * dc, dc)], go_v.at[i], lsem.at[i])
        src, dst = ((gate, gate_v), (up, up_v), (mas, mas_v), (mo1, m1_v), (mo2, m2_v))[i - C]
        return pltpu.make_async_copy(src, dst, lsem.at[i])

    for i in range(C + 5):
        local(i).start()

    barrier = pltpu.get_barrier_semaphore()
    for dev in peers:
        pl.semaphore_signal(barrier, inc=1, device_id=dev, device_id_type=MESH)

    tokens = ids.shape[1]
    hit0, hit1 = ids[0:1, :] == 0, ids[1:2, :] == 0
    chosen = jnp.where(hit0 | hit1, 1.0, 0.0)
    weight = jnp.where(hit0, probs[0:1, :], 0.0) + jnp.where(hit1, probs[1:2, :], 0.0)
    before = lax.broadcasted_iota(jnp.int32, (tokens, tokens), 0) < lax.broadcasted_iota(jnp.int32, (tokens, tokens), 1)
    count = jnp.dot(
        jnp.broadcast_to(chosen, (16, tokens)).astype(jnp.bfloat16),
        jnp.where(before, 1.0, 0.0).astype(jnp.bfloat16),
        preferred_element_type=jnp.float32,
    )
    slot = jnp.where(chosen > 0.5, count[0:1, :], -1.0)
    mark = lax.broadcasted_iota(jnp.int32, (cap, tokens), 0).astype(jnp.float32) == slot
    place[...] = jnp.where(mark, 1.0, 0.0).astype(jnp.bfloat16)
    wslot[...] = jnp.broadcast_to(jnp.sum(jnp.where(mark, weight, 0.0), axis=1, keepdims=True), wslot.shape)

    def block(c, y_, h_, lo=0, rows=None):
        e = y_ * NH + h_
        return G.at[c, pl.ds(pl.multiple_of(e * cap + lo, 32), cap if rows is None else rows), :]

    def copy(kind, c, src, dst, dev):
        return pltpu.make_async_remote_copy(
            src_ref=src, dst_ref=dst, send_sem=ssem.at[kind, c], recv_sem=rsem.at[kind, c],
            device_id=dev, device_id_type=MESH)

    def gather_copy(kind, c):
        if kind == 0:
            b, dev = block(c, y, zh), dev_z
        elif kind in (1, 2):
            b, dev = block(c, y, zh), (dev_yp if kind == 1 else dev_ym)
        elif kind in (3, 7):
            b, dev = block(c, ym, zh if kind == 3 else 1 - zh, 0, half), dev_yp
        elif kind in (4, 8):
            b, dev = block(c, yp, zh if kind == 4 else 1 - zh, half, half), dev_ym
        else:
            b, dev = block(c, y, 1 - zh), (dev_yp if kind == 5 else dev_ym)
        return copy(kind, c, b, b, dev)

    def gather_arrival(kind, c):
        if kind == 0:
            b = block(c, y, 1 - zh)
        elif kind in (1, 5):
            b = block(c, ym, zh if kind == 1 else 1 - zh)
        elif kind in (2, 6):
            b = block(c, yp, zh if kind == 2 else 1 - zh)
        elif kind in (3, 7):
            b = block(c, yo, zh if kind == 3 else 1 - zh, 0, half)
        else:
            b = block(c, yo, zh if kind == 4 else 1 - zh, half, half)
        return copy(kind, c, b, b, dev_z)

    def core_copy(c):
        return copy(9, c, csend.at[c], crecv.at[c], dev_c)

    def x_copy(c, k):
        return copy(9 + k, c, xsend.at[c, k - 1], xrecv.at[c, k - 1], dev_x[k - 1])

    def z_copy(c, k):
        return copy(12 + k, c, zsend.at[c, k - 1], zrecv.at[c, k - 1], dev_zl[k - 1])

    def fill(c):
        pltpu.make_async_copy(gout.at[:, pl.ds(0, dc)], go_v.at[c], lsem.at[c]).wait()
        rows = jnp.dot(place[...], go_v[c], preferred_element_type=jnp.float32)
        block(c, y, zh)[...] = (rows * wslot[:, 0:1]).astype(jnp.bfloat16)
        for kind in (0, 1, 2):
            gather_copy(kind, c).start()

    fill_first = min(AHEAD, C)
    pl.semaphore_wait(barrier, len(peers))
    for c in range(fill_first):
        fill(c)

    local(C).wait()
    local(C + 1).wait()

    def make_hidden(b, carry):
        cols = pl.ds(pl.multiple_of(b * 128, 128), 128)
        g = gate_v[:, cols].astype(jnp.float32)
        u = up_v[:, cols].astype(jnp.float32)
        h = (g / (1.0 + jnp.exp(-g)) * u).astype(jnp.bfloat16).T
        to = pl.multiple_of(b * 64, 64)
        H[0, pl.ds(to, 32), :] = h[0:32]
        H[1, pl.ds(to, 32), :] = h[32:64]
        H[0, pl.ds(to + 32, 32), :] = h[64:96]
        H[1, pl.ds(to + 32, 32), :] = h[96:128]
        return carry

    lax.fori_loop(0, gate_v.shape[1] // 128, make_hidden, 0)
    for i in range(2, 5):
        local(C + i).wait()
    ssum[...] = jnp.zeros_like(ssum)

    hrows = H.shape[1]
    xrows = hrows // NX
    zrows = xrows // NZ

    def stage_b(c):
        for kind in (1, 2):
            gather_arrival(kind, c).wait_recv()
            gather_copy(kind + 2, c).start()
        gather_arrival(0, c).wait_recv()
        for kind in (5, 6):
            gather_copy(kind, c).start()

    def stage_c(c):
        for kind in (5, 6):
            gather_arrival(kind, c).wait_recv()
            gather_copy(kind + 2, c).start()

    def stage_d(c):
        for kind in (3, 4, 7, 8):
            gather_arrival(kind, c).wait_recv()
        csend[c] = jnp.dot(H[1 - core], G[c], preferred_element_type=jnp.float32)
        core_copy(c).start()
        acc[...] = jnp.dot(H[core], G[c], preferred_element_type=jnp.float32)
        core_copy(c).wait_recv()
        for k in (2, 1, 3):
            base = ((x + k) % NX) * xrows

            def put(i, carry):
                rows = pl.ds(pl.multiple_of(base + i * TILE, TILE), TILE)
                encode(acc[rows, :] + crecv[c, rows, :], xsend.at[c, k - 1],
                       pl.ds(pl.multiple_of(i * TILE, TILE), TILE))
                return carry

            lax.fori_loop(0, xrows // TILE, put, 0)
            x_copy(c, k).start()

        own = pl.ds(pl.multiple_of(x * xrows, xrows), xrows)
        xacc[c] = acc[own, :] + crecv[c, own, :]

    def stage_e(c):
        for k in (1, 3, 2):
            x_copy(c, k).wait_recv()

        def join(i, carry):
            rows = pl.ds(pl.multiple_of(i * TILE, TILE), TILE)
            got = [decoded(xrecv.at[c, k - 1], rows) for k in range(1, NX)]
            for j in range(dc // 128):
                cols = slice(j * 128, (j + 1) * 128)
                total = xacc[c, rows, cols]
                for g in got:
                    total = total + g[j]
                xacc[c, rows, cols] = total
            return carry

        lax.fori_loop(0, xrows // TILE, join, 0)
        every = pl.ds(0, zrows)
        for k in (2, 1, 3):
            encode(xacc[c, pl.ds(pl.multiple_of(((zl + k) % NZ) * zrows, zrows), zrows), :], zsend.at[c, k - 1], every)
            z_copy(c, k).start()

    def stage_f(c):
        for k in (1, 3, 2):
            z_copy(c, k).wait_recv()
        g = xacc[c, pl.ds(pl.multiple_of(zl * zrows, zrows), zrows), :]
        got = [jnp.concatenate(decoded(zrecv.at[c, k - 1], pl.ds(0, zrows)), axis=1) for k in range(1, NZ)]
        for part in got:
            g = g + part
        cols = pl.ds(pl.multiple_of(c * dc, 128), dc)
        one = 0.9 * m1_v[:, cols] + 0.1 * g
        two = 0.95 * m2_v[:, cols] + 0.05 * g * g
        m1_o[:, cols] = one
        m2_o[:, cols] = two
        step = one / (1.0 - 0.9**20) / (jnp.sqrt(two / (1.0 - 0.95**20)) + 1e-08)
        step_v[:, cols] = step
        sq = step * step
        part = sq[:, 0:128]
        for j in range(1, dc // 128):
            part = part + sq[:, j * 128:(j + 1) * 128]
        ssum[...] += part

    def tick(t, carry):
        def guarded(stage, c):
            @pl.when((c >= 0) & (c < C))
            def _():
                stage(c)

        @pl.when(t + AHEAD < C)
        def _():
            fill(t + AHEAD)

        guarded(stage_b, t)
        guarded(stage_c, t - 1)
        guarded(stage_f, t - LAG_F)
        guarded(stage_e, t - LAG_E)
        guarded(stage_d, t - 2)
        return carry

    lax.fori_loop(0, C + LAG_F, tick, 0)

    mas2 = mas_v[...] * mas_v[...]
    wrms = jnp.sqrt(jnp.sum(mas2, axis=1, keepdims=True) / D + 1e-06)
    srms = jnp.sqrt(jnp.sum(ssum[...], axis=1, keepdims=True) / D + 1e-06)
    factor = jnp.minimum(1.0, 0.02 * wrms / (0.01 * srms))
    new = mas_v[...] - 0.01 * factor * step_v[...]
    nm_o[...] = new
    encode(new, own_q, pl.ds(0, own_rows))

    low = own_rows // 2
    dev_xp, dev_xm = dev_x[0], dev_x[NX - 2]

    def home(x_, z_, c_):
        return ((x_ % NX) * NZ + z_ % NZ) * NC + c_

    def piece(origin, part):
        if part is None:
            return q_o.at[origin]
        return q_o.at[origin, pl.ds(part * low, low), :]

    def send(i, src, dst, dev):
        return pltpu.make_async_remote_copy(
            src_ref=src, dst_ref=dst, send_sem=gs.at[i], recv_sem=gr.at[i], device_id=dev, device_id_type=MESH)

    sent = []

    def go(i, src, dst, dev):
        cp = send(i, src, dst, dev)
        cp.start()
        sent.append(cp)

    def arrived(i, dst):
        send(i, dst, dst, dev_c).wait_recv()

    Z0, XR, XF, CR = 0, 3, 11, 19

    def from_z(k):
        o = home(x, zl + NZ - k, core)
        arrived(Z0 + k - 1, piece(o, None))
        for d, dev in ((0, dev_xp), (1, dev_xm)):
            go(XR + d * 4 + k, piece(o, None), piece(o, None), dev)
        go(CR + k, piece(o, None), piece(o, None), dev_c)

    def from_x(k):
        for d, (off, dev) in enumerate(((NX - 1, dev_xp), (1, dev_xm))):
            o = home(x + off, zl + NZ - k, core)
            arrived(XR + d * 4 + k, piece(o, None))
            go(XF + d * 4 + k, piece(o, d), piece(o, d), dev)
            go(CR + off * 4 + k, piece(o, None), piece(o, None), dev_c)

    def from_far(k):
        o = home(x + 2, zl + NZ - k, core)
        for d in (0, 1):
            arrived(XF + d * 4 + k, piece(o, d))
        go(CR + 2 * 4 + k, piece(o, None), piece(o, None), dev_c)

    keep = pltpu.make_async_copy(own_q, q_o.at[dp], lsem.at[0])
    keep.start()
    go(XR, own_q, q_o.at[dp], dev_xp)
    go(XR + 4, own_q, q_o.at[dp], dev_xm)
    for k in (1, 3, 2):
        go(Z0 + k - 1, own_q, q_o.at[dp], dev_zl[k - 1])
    go(CR, own_q, q_o.at[dp], dev_c)
    from_z(1)
    from_z(3)
    from_x(0)
    from_z(2)
    for k in (1, 3, 2):
        from_x(k)
    for k in (0, 1, 3, 2):
        from_far(k)
    for off in (0, 1, 3, 2):
        for k in range(NZ):
            arrived(CR + off * 4 + k, piece(home(x + off, zl + NZ - k, 1 - core), None))
    for cp in sent:
        cp.wait_send()
    keep.wait()

    def drain(c, carry):
        for kind in range(9):
            gather_copy(kind, c).wait_send()
        core_copy(c).wait_send()
        for k in range(1, NX):
            x_copy(c, k).wait_send()
        for k in range(1, NZ):
            z_copy(c, k).wait_send()
        return carry

    lax.fori_loop(0, C, drain, 0)


def decode(q_ref, a_ref, b_ref, c_ref, o_ref, a_o, b_o, c_o):
    blocks, rows, width = q_ref.shape

    @pl.when(pl.program_id(0) == 0)
    def _():
        a_o[...] = a_ref[...]
        b_o[...] = b_ref[...]
        c_o[...] = c_ref[...]

    for b in range(blocks):
        for j, part in enumerate(decoded(q_ref.at[b], pl.ds(0, rows))):
            o_ref[pl.ds(b * rows, rows), j * 128:(j + 1) * 128] = part


def local(grad_out, expert_ids, gate_probs, saved_gate, saved_up, master, moment_one, moment_two):
    tokens, D = grad_out.shape
    cap = tokens * 3 // 8
    slots, _, width = saved_gate.shape
    rows = master.shape[1]
    devices = NX * NZ * NC
    C, dc = CHUNKS, D // CHUNKS
    f32, bf16, i16 = jnp.float32, jnp.bfloat16, jnp.int16
    vm = pl.BlockSpec(memory_space=pltpu.VMEM)
    hbm = pl.BlockSpec(memory_space=pl.ANY)
    hrows = width // NC
    xrows = hrows // NX
    outs = pl.pallas_call(
        kernel,
        name="step",
        out_shape=(
            jax.ShapeDtypeStruct((rows, D), f32),
            jax.ShapeDtypeStruct((rows, D), f32),
            jax.ShapeDtypeStruct((rows, D), f32),
            jax.ShapeDtypeStruct((devices, rows, D + 128), i16),
        ),
        in_specs=[vm, vm] + [hbm] * 6,
        out_specs=(vm, vm, vm, hbm),
        scratch_shapes=[
            pltpu.VMEM((C, tokens, dc), bf16),
            pltpu.VMEM((slots, width), bf16),
            pltpu.VMEM((slots, width), bf16),
            pltpu.VMEM((rows, D), f32),
            pltpu.VMEM((rows, D), f32),
            pltpu.VMEM((rows, D), f32),
            pltpu.VMEM((cap, tokens), bf16),
            pltpu.VMEM((cap, 128), f32),
            pltpu.VMEM((NC, hrows, slots), bf16),
            pltpu.VMEM((C, slots, dc), bf16),
            pltpu.VMEM((hrows, dc), f32),
            pltpu.VMEM((C, xrows, dc), f32),
            pltpu.VMEM((rows, D), f32),
            pltpu.VMEM((rows, 128), f32),
            pltpu.VMEM((C, hrows, dc), f32),
            pltpu.VMEM((C, hrows, dc), f32),
            pltpu.VMEM((C, NX - 1, xrows, dc + 128), i16),
            pltpu.VMEM((C, NX - 1, xrows, dc + 128), i16),
            pltpu.VMEM((C, NZ - 1, rows, dc + 128), i16),
            pltpu.VMEM((C, NZ - 1, rows, dc + 128), i16),
            pltpu.VMEM((rows, D + 128), i16),
            pltpu.SemaphoreType.DMA((C + 5,)),
            pltpu.SemaphoreType.DMA((16, C)),
            pltpu.SemaphoreType.DMA((16, C)),
            pltpu.SemaphoreType.DMA((35,)),
            pltpu.SemaphoreType.DMA((35,)),
        ],
        compiler_params=pltpu.CompilerParams(
            collective_id=0, has_side_effects=True, vmem_limit_bytes=60 << 20),
    )(
        expert_ids.T, gate_probs.T, grad_out,
        saved_gate.reshape(slots, width), saved_up.reshape(slots, width),
        master.reshape(rows, D), moment_one.reshape(rows, D), moment_two.reshape(rows, D),
    )
    new, one, two, q = outs
    per = 8
    whole = pl.BlockSpec((rows, D), lambda i: (0, 0))
    full, new, one, two = pl.pallas_call(
        decode,
        name="decode",
        grid=(devices // per,),
        out_shape=(jax.ShapeDtypeStruct((devices * rows, D), f32),) + (jax.ShapeDtypeStruct((rows, D), f32),) * 3,
        in_specs=[pl.BlockSpec((per, rows, D + 128), lambda i: (i, 0, 0)), whole, whole, whole],
        out_specs=(pl.BlockSpec((per * rows, D), lambda i: (i, 0)), whole, whole, whole),
    )(q, new, one, two)
    shape = master.shape
    return (new.reshape(shape), one.reshape(shape), two.reshape(shape), full.reshape(1, devices * rows, D))


def solution(mesh):
    return jax.shard_map(
        local,
        mesh=mesh,
        in_specs=(
            P(("dp", "expert"), None),
            P(("dp", "expert"), None),
            P(("dp", "expert"), None),
            P("dp", "expert", None),
            P("dp", "expert", None),
            P("expert", "dp", None),
            P("expert", "dp", None),
            P("expert", "dp", None),
        ),
        out_specs=(
            P("expert", "dp", None),
            P("expert", "dp", None),
            P("expert", "dp", None),
            P("expert", None, None),
        ),
        check_vma=False,
    )
```

```python
import functools

import jax
import jax.numpy as jnp
from jax import lax
from jax.experimental import pallas as pl
from jax.experimental.pallas import tpu as pltpu
from jax.sharding import PartitionSpec as P

MESH = pl.DeviceIdType.MESH
NX, NZ, NC, NY, NH = 4, 4, 2, 4, 2
CHUNKS = 12
AHEAD = 4
TILE = 32
LAG_R, LAG_E, LAG_F = 3, 5, 7
LEVELS = 32766.0
LOG2E = 1.4426950408889634
LN2 = 0.6931471805599453


def exponent(top):
    return jnp.floor(jnp.log(jnp.maximum(top, 1e-30)) * LOG2E) + 1.0


def encode(x, dst, rows):
    n = x.shape[-1] // 128
    parts = [x[:, j * 128:(j + 1) * 128] for j in range(n)]
    top = jnp.abs(parts[0])
    for p in parts[1:]:
        top = jnp.maximum(top, jnp.abs(p))
    e = exponent(top)
    s = jnp.exp(e * -LN2) * LEVELS
    for j, p in enumerate(parts):
        dst[rows, j * 128:(j + 1) * 128] = jnp.floor(p * s + 0.5).astype(jnp.int32).astype(jnp.int16)
    dst[rows, n * 128:] = e.astype(jnp.int32).astype(jnp.int16)


def decoded(src, rows):
    n = src.shape[-1] // 128 - 1
    s = jnp.exp(src[rows, n * 128:].astype(jnp.int32).astype(jnp.float32) * LN2) * (1.0 / LEVELS)
    return [src[rows, j * 128:(j + 1) * 128].astype(jnp.int32).astype(jnp.float32) * s for j in range(n)]


def kernel(ids, probs, gout, gate, up, mas, mo1, mo2, nm_o, m1_o, m2_o, q_o,
           go_v, gate_v, up_v, mas_v, m1_v, m2_v, place, wslot, H, G, acc, xacc, step_v, ssum,
           csend, crecv, xsend, xrecv, zsend, zrecv, own_q,
           lsem, ssem, rsem, gs, gr):
    dp = lax.axis_index("dp")
    ex = lax.axis_index("expert")
    core, zl, x = dp % NC, (dp // NC) % NZ, dp // (NC * NZ)
    y, zh = ex // NH, ex % NH
    cap = place.shape[0]
    half = cap // 2
    C, _, dc = go_v.shape
    own_rows, D = mas_v.shape

    def at(x_, z_, c_, y_, h_):
        return ((x_ * NZ + z_) * NC + c_, y_ * NH + h_)

    ym, yp = (y + NY - 1) % NY, (y + 1) % NY
    yo = (y + 2) % NY
    dev_z = at(x, zl, core, y, 1 - zh)
    dev_yp, dev_ym = at(x, zl, core, yp, zh), at(x, zl, core, ym, zh)
    dev_c = at(x, zl, 1 - core, y, zh)
    dev_x = [at((x + k) % NX, zl, core, y, zh) for k in range(1, NX)]
    dev_zl = [at(x, (zl + k) % NZ, core, y, zh) for k in range(1, NZ)]
    peers = [dev_z, dev_yp, dev_ym, dev_c] + dev_x + dev_zl

    def local(i):
        if i < C:
            return pltpu.make_async_copy(gout.at[:, pl.ds(i * dc, dc)], go_v.at[i], lsem.at[i])
        src, dst = ((gate, gate_v), (up, up_v), (mas, mas_v), (mo1, m1_v), (mo2, m2_v))[i - C]
        return pltpu.make_async_copy(src, dst, lsem.at[i])

    fill_first = min(AHEAD, C)
    for i in range(fill_first):
        local(i).start()

    barrier = pltpu.get_barrier_semaphore()
    for dev in peers:
        pl.semaphore_signal(barrier, inc=1, device_id=dev, device_id_type=MESH)

    tokens = ids.shape[1]
    hit0, hit1 = ids[0:1, :] == 0, ids[1:2, :] == 0
    chosen = jnp.where(hit0 | hit1, 1.0, 0.0)
    weight = jnp.where(hit0, probs[0:1, :], 0.0) + jnp.where(hit1, probs[1:2, :], 0.0)
    before = lax.broadcasted_iota(jnp.int32, (tokens, tokens), 0) < lax.broadcasted_iota(jnp.int32, (tokens, tokens), 1)
    count = jnp.dot(
        jnp.broadcast_to(chosen, (16, tokens)).astype(jnp.bfloat16),
        jnp.where(before, 1.0, 0.0).astype(jnp.bfloat16),
        preferred_element_type=jnp.float32,
    )
    slot = jnp.where(chosen > 0.5, count[0:1, :], -1.0)
    mark = lax.broadcasted_iota(jnp.int32, (cap, tokens), 0).astype(jnp.float32) == slot
    place[...] = jnp.where(mark, 1.0, 0.0).astype(jnp.bfloat16)
    wslot[...] = jnp.broadcast_to(jnp.sum(jnp.where(mark, weight, 0.0), axis=1, keepdims=True), wslot.shape)

    def block(c, y_, h_, lo=0, rows=None):
        e = y_ * NH + h_
        return G.at[c, pl.ds(pl.multiple_of(e * cap + lo, 32), cap if rows is None else rows), :]

    def copy(kind, c, src, dst, dev):
        return pltpu.make_async_remote_copy(
            src_ref=src, dst_ref=dst, send_sem=ssem.at[kind, c], recv_sem=rsem.at[kind, c],
            device_id=dev, device_id_type=MESH)

    def gather_copy(kind, c):
        if kind == 0:
            b, dev = block(c, y, zh), dev_z
        elif kind in (1, 2):
            b, dev = block(c, y, zh), (dev_yp if kind == 1 else dev_ym)
        elif kind in (3, 7):
            b, dev = block(c, ym, zh if kind == 3 else 1 - zh, 0, half), dev_yp
        elif kind in (4, 8):
            b, dev = block(c, yp, zh if kind == 4 else 1 - zh, half, half), dev_ym
        else:
            b, dev = block(c, y, 1 - zh), (dev_yp if kind == 5 else dev_ym)
        return copy(kind, c, b, b, dev)

    def gather_arrival(kind, c):
        if kind == 0:
            b = block(c, y, 1 - zh)
        elif kind in (1, 5):
            b = block(c, ym, zh if kind == 1 else 1 - zh)
        elif kind in (2, 6):
            b = block(c, yp, zh if kind == 2 else 1 - zh)
        elif kind in (3, 7):
            b = block(c, yo, zh if kind == 3 else 1 - zh, 0, half)
        else:
            b = block(c, yo, zh if kind == 4 else 1 - zh, half, half)
        return copy(kind, c, b, b, dev_z)

    def core_copy(c):
        return copy(9, c, csend.at[c], crecv.at[c], dev_c)

    def x_copy(c, k):
        return copy(9 + k, c, xsend.at[c, k - 1], xrecv.at[c, k - 1], dev_x[k - 1])

    def z_copy(c, k):
        return copy(12 + k, c, zsend.at[c, k - 1], zrecv.at[c, k - 1], dev_zl[k - 1])

    def fill(c):
        pltpu.make_async_copy(gout.at[:, pl.ds(0, dc)], go_v.at[c], lsem.at[c]).wait()
        rows = jnp.dot(place[...], go_v[c], preferred_element_type=jnp.float32)
        block(c, y, zh)[...] = (rows * wslot[:, 0:1]).astype(jnp.bfloat16)
        for kind in (0, 1, 2):
            gather_copy(kind, c).start()

    pl.semaphore_wait(barrier, len(peers))
    for c in range(fill_first):
        fill(c)
        if c == 0:
            for i in [C, C + 1] + list(range(fill_first, C)) + [C + 2, C + 3, C + 4]:
                local(i).start()

    local(C).wait()
    local(C + 1).wait()

    def make_hidden(b, carry):
        cols = pl.ds(pl.multiple_of(b * 128, 128), 128)
        g = gate_v[:, cols].astype(jnp.float32)
        u = up_v[:, cols].astype(jnp.float32)
        h = (g / (1.0 + jnp.exp(-g)) * u).astype(jnp.bfloat16).T
        to = pl.multiple_of(b * 64, 64)
        H[0, pl.ds(to, 32), :] = h[0:32]
        H[1, pl.ds(to, 32), :] = h[32:64]
        H[0, pl.ds(to + 32, 32), :] = h[64:96]
        H[1, pl.ds(to + 32, 32), :] = h[96:128]
        return carry

    lax.fori_loop(0, gate_v.shape[1] // 128, make_hidden, 0)
    for i in range(2, 5):
        local(C + i).wait()
    ssum[...] = jnp.zeros_like(ssum)

    hrows = H.shape[1]
    xrows = hrows // NX
    zrows = xrows // NZ

    def stage_b(c):
        for kind in (1, 2):
            gather_arrival(kind, c).wait_recv()
            gather_copy(kind + 2, c).start()
        gather_arrival(0, c).wait_recv()
        for kind in (5, 6):
            gather_copy(kind, c).start()

    def stage_c(c):
        for kind in (5, 6):
            gather_arrival(kind, c).wait_recv()
            gather_copy(kind + 2, c).start()

    def stage_d(c):
        for kind in (3, 4, 7, 8):
            gather_arrival(kind, c).wait_recv()
        csend[c] = jnp.dot(H[1 - core], G[c], preferred_element_type=jnp.float32)
        core_copy(c).start()
        acc[c % 2] = jnp.dot(H[core], G[c], preferred_element_type=jnp.float32)

    def stage_r(c):
        core_copy(c).wait_recv()
        for k in (2, 1, 3):
            base = ((x + k) % NX) * xrows

            def put(i, carry):
                rows = pl.ds(pl.multiple_of(base + i * TILE, TILE), TILE)
                encode(acc[c % 2, rows, :] + crecv[c, rows, :], xsend.at[c, k - 1],
                       pl.ds(pl.multiple_of(i * TILE, TILE), TILE))
                return carry

            lax.fori_loop(0, xrows // TILE, put, 0)
            x_copy(c, k).start()

        own = pl.ds(pl.multiple_of(x * xrows, xrows), xrows)
        xacc[c] = acc[c % 2, own, :] + crecv[c, own, :]

    def stage_e(c):
        for k in (1, 3, 2):
            x_copy(c, k).wait_recv()

        def join(i, carry):
            rows = pl.ds(pl.multiple_of(i * TILE, TILE), TILE)
            got = [decoded(xrecv.at[c, k - 1], rows) for k in range(1, NX)]
            for j in range(dc // 128):
                cols = slice(j * 128, (j + 1) * 128)
                total = xacc[c, rows, cols]
                for g in got:
                    total = total + g[j]
                xacc[c, rows, cols] = total
            return carry

        lax.fori_loop(0, xrows // TILE, join, 0)
        every = pl.ds(0, zrows)
        for k in (2, 1, 3):
            encode(xacc[c, pl.ds(pl.multiple_of(((zl + k) % NZ) * zrows, zrows), zrows), :], zsend.at[c, k - 1], every)
            z_copy(c, k).start()

    def stage_f(c):
        for k in (1, 3, 2):
            z_copy(c, k).wait_recv()
        g = xacc[c, pl.ds(pl.multiple_of(zl * zrows, zrows), zrows), :]
        got = [jnp.concatenate(decoded(zrecv.at[c, k - 1], pl.ds(0, zrows)), axis=1) for k in range(1, NZ)]
        for part in got:
            g = g + part
        cols = pl.ds(pl.multiple_of(c * dc, 128), dc)
        one = 0.9 * m1_v[:, cols] + 0.1 * g
        two = 0.95 * m2_v[:, cols] + 0.05 * g * g
        m1_o[:, cols] = one
        m2_o[:, cols] = two
        step = one / (1.0 - 0.9**20) / (jnp.sqrt(two / (1.0 - 0.95**20)) + 1e-08)
        step_v[:, cols] = step
        sq = step * step
        part = sq[:, 0:128]
        for j in range(1, dc // 128):
            part = part + sq[:, j * 128:(j + 1) * 128]
        ssum[...] += part

    def tick(t, carry):
        def guarded(stage, c):
            @pl.when((c >= 0) & (c < C))
            def _():
                stage(c)

        @pl.when(t + AHEAD < C)
        def _():
            fill(t + AHEAD)

        guarded(stage_b, t)
        guarded(stage_c, t - 1)
        guarded(stage_f, t - LAG_F)
        guarded(stage_e, t - LAG_E)
        guarded(stage_r, t - LAG_R)
        guarded(stage_d, t - 2)
        return carry

    lax.fori_loop(0, C + LAG_F, tick, 0)

    mas2 = mas_v[...] * mas_v[...]
    wrms = jnp.sqrt(jnp.sum(mas2, axis=1, keepdims=True) / D + 1e-06)
    srms = jnp.sqrt(jnp.sum(ssum[...], axis=1, keepdims=True) / D + 1e-06)
    factor = jnp.minimum(1.0, 0.02 * wrms / (0.01 * srms))
    new = mas_v[...] - 0.01 * factor * step_v[...]
    nm_o[...] = new
    encode(new, own_q, pl.ds(0, own_rows))

    low = own_rows // 2
    dev_xp, dev_xm = dev_x[0], dev_x[NX - 2]

    def home(x_, z_, c_):
        return ((x_ % NX) * NZ + z_ % NZ) * NC + c_

    def piece(origin, part):
        if part is None:
            return q_o.at[origin]
        return q_o.at[origin, pl.ds(part * low, low), :]

    def send(i, src, dst, dev):
        return pltpu.make_async_remote_copy(
            src_ref=src, dst_ref=dst, send_sem=gs.at[i], recv_sem=gr.at[i], device_id=dev, device_id_type=MESH)

    sent = []

    def go(i, src, dst, dev):
        cp = send(i, src, dst, dev)
        cp.start()
        sent.append(cp)

    def arrived(i, dst):
        send(i, dst, dst, dev_c).wait_recv()

    Z0, XR, XF, CR = 0, 3, 11, 19

    def from_z(k):
        o = home(x, zl + NZ - k, core)
        arrived(Z0 + k - 1, piece(o, None))
        for d, dev in ((0, dev_xp), (1, dev_xm)):
            go(XR + d * 4 + k, piece(o, None), piece(o, None), dev)
        go(CR + k, piece(o, None), piece(o, None), dev_c)

    def from_x(k):
        for d, (off, dev) in enumerate(((NX - 1, dev_xp), (1, dev_xm))):
            o = home(x + off, zl + NZ - k, core)
            arrived(XR + d * 4 + k, piece(o, None))
            go(XF + d * 4 + k, piece(o, d), piece(o, d), dev)
            go(CR + off * 4 + k, piece(o, None), piece(o, None), dev_c)

    def from_far(k):
        o = home(x + 2, zl + NZ - k, core)
        for d in (0, 1):
            arrived(XF + d * 4 + k, piece(o, d))
        go(CR + 2 * 4 + k, piece(o, None), piece(o, None), dev_c)

    go(XR, own_q, q_o.at[dp], dev_xp)
    go(XR + 4, own_q, q_o.at[dp], dev_xm)
    for k in (1, 3, 2):
        go(Z0 + k - 1, own_q, q_o.at[dp], dev_zl[k - 1])
    go(CR, own_q, q_o.at[dp], dev_c)
    kept = [pltpu.make_async_copy(own_q, q_o.at[dp], lsem.at[0])]
    for cp in kept:
        cp.start()
    from_z(1)
    from_z(3)
    from_x(0)
    from_z(2)
    for k in (1, 3, 2):
        from_x(k)
    for k in (0, 1, 3, 2):
        from_far(k)
    for off in (0, 1, 3, 2):
        for k in range(NZ):
            arrived(CR + off * 4 + k, piece(home(x + off, zl + NZ - k, 1 - core), None))
    for cp in sent:
        cp.wait_send()
    for cp in kept:
        cp.wait()

    def drain(c, carry):
        for kind in range(9):
            gather_copy(kind, c).wait_send()
        core_copy(c).wait_send()
        for k in range(1, NX):
            x_copy(c, k).wait_send()
        for k in range(1, NZ):
            z_copy(c, k).wait_send()
        return carry

    lax.fori_loop(0, C, drain, 0)


def decode(q_ref, a_ref, b_ref, c_ref, o_ref, a_o, b_o, c_o):
    blocks, rows, width = q_ref.shape

    @pl.when(pl.program_id(0) == 0)
    def _():
        a_o[...] = a_ref[...]
        b_o[...] = b_ref[...]
        c_o[...] = c_ref[...]

    blocks = o_ref.shape[0] // rows
    for b in range(blocks):
        for j, part in enumerate(decoded(q_ref.at[pl.program_id(0) * blocks + b], pl.ds(0, rows))):
            o_ref[pl.ds(b * rows, rows), j * 128:(j + 1) * 128] = part


def local(grad_out, expert_ids, gate_probs, saved_gate, saved_up, master, moment_one, moment_two):
    tokens, D = grad_out.shape
    cap = tokens * 3 // 8
    slots, _, width = saved_gate.shape
    rows = master.shape[1]
    devices = NX * NZ * NC
    C, dc = CHUNKS, D // CHUNKS
    f32, bf16, i16 = jnp.float32, jnp.bfloat16, jnp.int16
    vm = pl.BlockSpec(memory_space=pltpu.VMEM)
    hbm = pl.BlockSpec(memory_space=pl.ANY)
    hrows = width // NC
    xrows = hrows // NX
    outs = pl.pallas_call(
        kernel,
        name="step",
        out_shape=(
            pltpu.VMEM((rows, D), f32),
            pltpu.VMEM((rows, D), f32),
            pltpu.VMEM((rows, D), f32),
            pltpu.VMEM((devices, rows, D + 128), i16),
        ),
        in_specs=[vm, vm] + [hbm] * 6,
        out_specs=(vm, vm, vm, vm),
        scratch_shapes=[
            pltpu.VMEM((C, tokens, dc), bf16),
            pltpu.VMEM((slots, width), bf16),
            pltpu.VMEM((slots, width), bf16),
            pltpu.VMEM((rows, D), f32),
            pltpu.VMEM((rows, D), f32),
            pltpu.VMEM((rows, D), f32),
            pltpu.VMEM((cap, tokens), bf16),
            pltpu.VMEM((cap, 128), f32),
            pltpu.VMEM((NC, hrows, slots), bf16),
            pltpu.VMEM((C, slots, dc), bf16),
            pltpu.VMEM((2, hrows, dc), f32),
            pltpu.VMEM((C, xrows, dc), f32),
            pltpu.VMEM((rows, D), f32),
            pltpu.VMEM((rows, 128), f32),
            pltpu.VMEM((C, hrows, dc), f32),
            pltpu.VMEM((C, hrows, dc), f32),
            pltpu.VMEM((C, NX - 1, xrows, dc + 128), i16),
            pltpu.VMEM((C, NX - 1, xrows, dc + 128), i16),
            pltpu.VMEM((C, NZ - 1, rows, dc + 128), i16),
            pltpu.VMEM((C, NZ - 1, rows, dc + 128), i16),
            pltpu.VMEM((rows, D + 128), i16),
            pltpu.SemaphoreType.DMA((C + 5,)),
            pltpu.SemaphoreType.DMA((16, C)),
            pltpu.SemaphoreType.DMA((16, C)),
            pltpu.SemaphoreType.DMA((35,)),
            pltpu.SemaphoreType.DMA((35,)),
        ],
        compiler_params=pltpu.CompilerParams(
            collective_id=0, has_side_effects=True, vmem_limit_bytes=54 << 20),
    )(
        expert_ids.T, gate_probs.T, grad_out,
        saved_gate.reshape(slots, width), saved_up.reshape(slots, width),
        master.reshape(rows, D), moment_one.reshape(rows, D), moment_two.reshape(rows, D),
    )
    new, one, two, q = outs
    per = 4
    whole = pl.BlockSpec((rows, D), lambda i: (0, 0))
    full, new, one, two = pl.pallas_call(
        decode,
        name="decode",
        grid=(devices // per,),
        out_shape=(jax.ShapeDtypeStruct((devices * rows, D), f32),) + (jax.ShapeDtypeStruct((rows, D), f32),) * 3,
        in_specs=[vm, vm, vm, vm],
        out_specs=(pl.BlockSpec((per * rows, D), lambda i: (i, 0)), whole, whole, whole),
        compiler_params=pltpu.CompilerParams(vmem_limit_bytes=24 << 20),
    )(q, new, one, two)
    shape = master.shape
    return (new.reshape(shape), one.reshape(shape), two.reshape(shape), full.reshape(1, devices * rows, D))


def solution(mesh):
    return jax.shard_map(
        local,
        mesh=mesh,
        in_specs=(
            P(("dp", "expert"), None),
            P(("dp", "expert"), None),
            P(("dp", "expert"), None),
            P("dp", "expert", None),
            P("dp", "expert", None),
            P("expert", "dp", None),
            P("expert", "dp", None),
            P("expert", "dp", None),
        ),
        out_specs=(
            P("expert", "dp", None),
            P("expert", "dp", None),
            P("expert", "dp", None),
            P("expert", None, None),
        ),
        check_vma=False,
    )
```

```python
import functools

import jax
import jax.numpy as jnp
from jax import lax
from jax.experimental import pallas as pl
from jax.experimental.pallas import tpu as pltpu
from jax.sharding import PartitionSpec as P

MESH = pl.DeviceIdType.MESH
NX, NZ, NC, NY, NH = 4, 4, 2, 4, 2
CHUNKS = 12
AHEAD = 4
TILE = 32
LAG_R, LAG_E, LAG_F = 3, 5, 7
LEVELS = 32766.0
LOG2E = 1.4426950408889634
LN2 = 0.6931471805599453


def exponent(top):
    return jnp.floor(jnp.log(jnp.maximum(top, 1e-30)) * LOG2E) + 1.0


def encode(x, dst, rows):
    n = x.shape[-1] // 128
    parts = [x[:, j * 128:(j + 1) * 128] for j in range(n)]
    top = jnp.abs(parts[0])
    for p in parts[1:]:
        top = jnp.maximum(top, jnp.abs(p))
    e = exponent(top)
    s = jnp.exp(e * -LN2) * LEVELS
    for j, p in enumerate(parts):
        dst[rows, j * 128:(j + 1) * 128] = jnp.floor(p * s + 0.5).astype(jnp.int32).astype(jnp.int16)
    dst[rows, n * 128:] = e.astype(jnp.int32).astype(jnp.int16)


def decoded(src, rows):
    n = src.shape[-1] // 128 - 1
    s = jnp.exp(src[rows, n * 128:].astype(jnp.int32).astype(jnp.float32) * LN2) * (1.0 / LEVELS)
    return [src[rows, j * 128:(j + 1) * 128].astype(jnp.int32).astype(jnp.float32) * s for j in range(n)]


def kernel(ids, probs, gout, gate, up, mas, mo1, mo2, nm_o, m1_o, m2_o, q_o,
           go_v, gate_v, up_v, mas_v, m1_v, m2_v, place, wslot, H, G, acc, xacc, step_v, ssum, wrms_v,
           csend, crecv, xsend, xrecv, zsend, zrecv, own_q,
           lsem, ssem, rsem, gs, gr):
    dp = lax.axis_index("dp")
    ex = lax.axis_index("expert")
    core, zl, x = dp % NC, (dp // NC) % NZ, dp // (NC * NZ)
    y, zh = ex // NH, ex % NH
    cap = place.shape[0]
    half = cap // 2
    C, _, dc = go_v.shape
    own_rows, D = mas_v.shape

    def at(x_, z_, c_, y_, h_):
        return ((x_ * NZ + z_) * NC + c_, y_ * NH + h_)

    ym, yp = (y + NY - 1) % NY, (y + 1) % NY
    yo = (y + 2) % NY
    dev_z = at(x, zl, core, y, 1 - zh)
    dev_yp, dev_ym = at(x, zl, core, yp, zh), at(x, zl, core, ym, zh)
    dev_c = at(x, zl, 1 - core, y, zh)
    dev_x = [at((x + k) % NX, zl, core, y, zh) for k in range(1, NX)]
    dev_zl = [at(x, (zl + k) % NZ, core, y, zh) for k in range(1, NZ)]
    peers = [dev_z, dev_yp, dev_ym, dev_c] + dev_x + dev_zl

    def local(i):
        if i < C:
            return pltpu.make_async_copy(gout.at[:, pl.ds(i * dc, dc)], go_v.at[i], lsem.at[i])
        src, dst = ((gate, gate_v), (up, up_v), (mas, mas_v), (mo1, m1_v), (mo2, m2_v))[i - C]
        return pltpu.make_async_copy(src, dst, lsem.at[i])

    fill_first = min(AHEAD, C)
    for i in range(fill_first):
        local(i).start()

    barrier = pltpu.get_barrier_semaphore()
    for dev in peers:
        pl.semaphore_signal(barrier, inc=1, device_id=dev, device_id_type=MESH)

    tokens = ids.shape[1]
    hit0, hit1 = ids[0:1, :] == 0, ids[1:2, :] == 0
    chosen = jnp.where(hit0 | hit1, 1.0, 0.0)
    weight = jnp.where(hit0, probs[0:1, :], 0.0) + jnp.where(hit1, probs[1:2, :], 0.0)
    before = lax.broadcasted_iota(jnp.int32, (tokens, tokens), 0) < lax.broadcasted_iota(jnp.int32, (tokens, tokens), 1)
    count = jnp.dot(
        jnp.broadcast_to(chosen, (16, tokens)).astype(jnp.bfloat16),
        jnp.where(before, 1.0, 0.0).astype(jnp.bfloat16),
        preferred_element_type=jnp.float32,
    )
    slot = jnp.where(chosen > 0.5, count[0:1, :], -1.0)
    mark = lax.broadcasted_iota(jnp.int32, (cap, tokens), 0).astype(jnp.float32) == slot
    place[...] = jnp.where(mark, 1.0, 0.0).astype(jnp.bfloat16)
    wslot[...] = jnp.broadcast_to(jnp.sum(jnp.where(mark, weight, 0.0), axis=1, keepdims=True), wslot.shape)

    def block(c, y_, h_, lo=0, rows=None):
        e = y_ * NH + h_
        return G.at[c, pl.ds(pl.multiple_of(e * cap + lo, 32), cap if rows is None else rows), :]

    def copy(kind, c, src, dst, dev):
        return pltpu.make_async_remote_copy(
            src_ref=src, dst_ref=dst, send_sem=ssem.at[kind, c], recv_sem=rsem.at[kind, c],
            device_id=dev, device_id_type=MESH)

    def gather_copy(kind, c):
        if kind == 0:
            b, dev = block(c, y, zh), dev_z
        elif kind in (1, 2):
            b, dev = block(c, y, zh), (dev_yp if kind == 1 else dev_ym)
        elif kind in (3, 7):
            b, dev = block(c, ym, zh if kind == 3 else 1 - zh, 0, half), dev_yp
        elif kind in (4, 8):
            b, dev = block(c, yp, zh if kind == 4 else 1 - zh, half, half), dev_ym
        else:
            b, dev = block(c, y, 1 - zh), (dev_yp if kind == 5 else dev_ym)
        return copy(kind, c, b, b, dev)

    def gather_arrival(kind, c):
        if kind == 0:
            b = block(c, y, 1 - zh)
        elif kind in (1, 5):
            b = block(c, ym, zh if kind == 1 else 1 - zh)
        elif kind in (2, 6):
            b = block(c, yp, zh if kind == 2 else 1 - zh)
        elif kind in (3, 7):
            b = block(c, yo, zh if kind == 3 else 1 - zh, 0, half)
        else:
            b = block(c, yo, zh if kind == 4 else 1 - zh, half, half)
        return copy(kind, c, b, b, dev_z)

    def core_copy(c):
        return copy(9, c, csend.at[c], crecv.at[c], dev_c)

    def x_copy(c, k):
        return copy(9 + k, c, xsend.at[c, k - 1], xrecv.at[c, k - 1], dev_x[k - 1])

    def z_copy(c, k):
        return copy(12 + k, c, zsend.at[c, k - 1], zrecv.at[c, k - 1], dev_zl[k - 1])

    def fill(c):
        pltpu.make_async_copy(gout.at[:, pl.ds(0, dc)], go_v.at[c], lsem.at[c]).wait()
        rows = jnp.dot(place[...], go_v[c], preferred_element_type=jnp.float32)
        block(c, y, zh)[...] = (rows * wslot[:, 0:1]).astype(jnp.bfloat16)
        for kind in (0, 1, 2):
            gather_copy(kind, c).start()

    pl.semaphore_wait(barrier, len(peers))
    for c in range(fill_first):
        fill(c)
        if c == 0:
            for i in [C, C + 1] + list(range(fill_first, C)) + [C + 2, C + 3, C + 4]:
                local(i).start()

    local(C).wait()
    local(C + 1).wait()

    def make_hidden(b, carry):
        cols = pl.ds(pl.multiple_of(b * 128, 128), 128)
        g = gate_v[:, cols].astype(jnp.float32)
        u = up_v[:, cols].astype(jnp.float32)
        h = (g / (1.0 + jnp.exp(-g)) * u).astype(jnp.bfloat16).T
        to = pl.multiple_of(b * 64, 64)
        H[0, pl.ds(to, 32), :] = h[0:32]
        H[1, pl.ds(to, 32), :] = h[32:64]
        H[0, pl.ds(to + 32, 32), :] = h[64:96]
        H[1, pl.ds(to + 32, 32), :] = h[96:128]
        return carry

    lax.fori_loop(0, gate_v.shape[1] // 128, make_hidden, 0)
    for i in range(2, 5):
        local(C + i).wait()
    ssum[...] = jnp.zeros_like(ssum)
    mas2 = mas_v[...] * mas_v[...]
    wrms_v[...] = jnp.broadcast_to(jnp.sqrt(jnp.sum(mas2, axis=1, keepdims=True) / D + 1e-06), wrms_v.shape)

    hrows = H.shape[1]
    xrows = hrows // NX
    zrows = xrows // NZ

    def stage_b(c):
        for kind in (1, 2):
            gather_arrival(kind, c).wait_recv()
            gather_copy(kind + 2, c).start()
        gather_arrival(0, c).wait_recv()
        for kind in (5, 6):
            gather_copy(kind, c).start()

    def stage_c(c):
        for kind in (5, 6):
            gather_arrival(kind, c).wait_recv()
            gather_copy(kind + 2, c).start()

    def stage_d(c):
        for kind in (3, 4, 7, 8):
            gather_arrival(kind, c).wait_recv()
        csend[c] = jnp.dot(H[1 - core], G[c], preferred_element_type=jnp.float32)
        core_copy(c).start()
        acc[c % 2] = jnp.dot(H[core], G[c], preferred_element_type=jnp.float32)

    def stage_r(c):
        core_copy(c).wait_recv()
        for k in (2, 1, 3):
            base = ((x + k) % NX) * xrows

            def put(i, carry):
                rows = pl.ds(pl.multiple_of(base + i * TILE, TILE), TILE)
                encode(acc[c % 2, rows, :] + crecv[c, rows, :], xsend.at[c, k - 1],
                       pl.ds(pl.multiple_of(i * TILE, TILE), TILE))
                return carry

            lax.fori_loop(0, xrows // TILE, put, 0, unroll=True)
            x_copy(c, k).start()

        own = pl.ds(pl.multiple_of(x * xrows, xrows), xrows)
        xacc[c] = acc[c % 2, own, :] + crecv[c, own, :]

    def stage_e(c):
        for k in (1, 3, 2):
            x_copy(c, k).wait_recv()

        def join(i, carry):
            rows = pl.ds(pl.multiple_of(i * TILE, TILE), TILE)
            got = [decoded(xrecv.at[c, k - 1], rows) for k in range(1, NX)]
            for j in range(dc // 128):
                cols = slice(j * 128, (j + 1) * 128)
                total = xacc[c, rows, cols]
                for g in got:
                    total = total + g[j]
                xacc[c, rows, cols] = total
            return carry

        lax.fori_loop(0, xrows // TILE, join, 0, unroll=True)
        every = pl.ds(0, zrows)
        for k in (2, 1, 3):
            encode(xacc[c, pl.ds(pl.multiple_of(((zl + k) % NZ) * zrows, zrows), zrows), :], zsend.at[c, k - 1], every)
            z_copy(c, k).start()

    def stage_f(c):
        for k in (1, 3, 2):
            z_copy(c, k).wait_recv()
        g = xacc[c, pl.ds(pl.multiple_of(zl * zrows, zrows), zrows), :]
        got = [jnp.concatenate(decoded(zrecv.at[c, k - 1], pl.ds(0, zrows)), axis=1) for k in range(1, NZ)]
        for part in got:
            g = g + part
        cols = pl.ds(pl.multiple_of(c * dc, 128), dc)
        one = 0.9 * m1_v[:, cols] + 0.1 * g
        two = 0.95 * m2_v[:, cols] + 0.05 * g * g
        m1_o[:, cols] = one
        m2_o[:, cols] = two
        step = one / (1.0 - 0.9**20) / (jnp.sqrt(two / (1.0 - 0.95**20)) + 1e-08)
        step_v[:, cols] = step
        sq = step * step
        part = sq[:, 0:128]
        for j in range(1, dc // 128):
            part = part + sq[:, j * 128:(j + 1) * 128]
        ssum[...] += part

    def tick(t, carry):
        def guarded(stage, c):
            @pl.when((c >= 0) & (c < C))
            def _():
                stage(c)

        @pl.when(t + AHEAD < C)
        def _():
            fill(t + AHEAD)

        guarded(stage_b, t)
        guarded(stage_c, t - 1)
        guarded(stage_f, t - LAG_F)
        guarded(stage_e, t - LAG_E)
        guarded(stage_r, t - LAG_R)
        guarded(stage_d, t - 2)
        return carry

    lax.fori_loop(0, C + LAG_F, tick, 0)

    wrms = wrms_v[:, 0:1]
    srms = jnp.sqrt(jnp.sum(ssum[...], axis=1, keepdims=True) / D + 1e-06)
    factor = jnp.minimum(1.0, 0.02 * wrms / (0.01 * srms))
    new = mas_v[...] - 0.01 * factor * step_v[...]
    nm_o[...] = new
    encode(new, own_q, pl.ds(0, own_rows))

    low = own_rows // 2
    dev_xp, dev_xm = dev_x[0], dev_x[NX - 2]

    def home(x_, z_, c_):
        return ((x_ % NX) * NZ + z_ % NZ) * NC + c_

    def piece(origin, part):
        if part is None:
            return q_o.at[origin]
        return q_o.at[origin, pl.ds(part * low, low), :]

    def send(i, src, dst, dev):
        return pltpu.make_async_remote_copy(
            src_ref=src, dst_ref=dst, send_sem=gs.at[i], recv_sem=gr.at[i], device_id=dev, device_id_type=MESH)

    sent = []

    def go(i, src, dst, dev):
        cp = send(i, src, dst, dev)
        cp.start()
        sent.append(cp)

    def arrived(i, dst):
        send(i, dst, dst, dev_c).wait_recv()

    Z0, XR, XF, CR = 0, 3, 11, 19

    def from_z(k):
        o = home(x, zl + NZ - k, core)
        arrived(Z0 + k - 1, piece(o, None))
        for d, dev in ((0, dev_xp), (1, dev_xm)):
            go(XR + d * 4 + k, piece(o, None), piece(o, None), dev)
        go(CR + k, piece(o, None), piece(o, None), dev_c)

    def from_x(k):
        for d, (off, dev) in enumerate(((NX - 1, dev_xp), (1, dev_xm))):
            o = home(x + off, zl + NZ - k, core)
            arrived(XR + d * 4 + k, piece(o, None))
            go(XF + d * 4 + k, piece(o, d), piece(o, d), dev)
            go(CR + off * 4 + k, piece(o, None), piece(o, None), dev_c)

    def from_far(k):
        o = home(x + 2, zl + NZ - k, core)
        for d in (0, 1):
            arrived(XF + d * 4 + k, piece(o, d))
        go(CR + 2 * 4 + k, piece(o, None), piece(o, None), dev_c)

    go(XR, own_q, q_o.at[dp], dev_xp)
    go(XR + 4, own_q, q_o.at[dp], dev_xm)
    for k in (1, 3, 2):
        go(Z0 + k - 1, own_q, q_o.at[dp], dev_zl[k - 1])
    go(CR, own_q, q_o.at[dp], dev_c)
    kept = [pltpu.make_async_copy(own_q, q_o.at[dp], lsem.at[0])]
    for cp in kept:
        cp.start()
    from_z(1)
    from_z(3)
    from_x(0)
    from_z(2)
    for k in (1, 3, 2):
        from_x(k)
    for k in (0, 1, 3, 2):
        from_far(k)
    for off in (0, 1, 3, 2):
        for k in range(NZ):
            arrived(CR + off * 4 + k, piece(home(x + off, zl + NZ - k, 1 - core), None))
    for cp in sent:
        cp.wait_send()
    for cp in kept:
        cp.wait()

    def drain(c, carry):
        for kind in range(9):
            gather_copy(kind, c).wait_send()
        core_copy(c).wait_send()
        for k in range(1, NX):
            x_copy(c, k).wait_send()
        for k in range(1, NZ):
            z_copy(c, k).wait_send()
        return carry

    lax.fori_loop(0, C, drain, 0)


def decode(q_ref, a_ref, b_ref, c_ref, o_ref, a_o, b_o, c_o):
    blocks, rows, width = q_ref.shape

    @pl.when(pl.program_id(0) == 0)
    def _():
        a_o[...] = a_ref[...]
        b_o[...] = b_ref[...]
        c_o[...] = c_ref[...]

    blocks = o_ref.shape[0] // rows
    for b in range(blocks):
        for j, part in enumerate(decoded(q_ref.at[pl.program_id(0) * blocks + b], pl.ds(0, rows))):
            o_ref[pl.ds(b * rows, rows), j * 128:(j + 1) * 128] = part


def local(grad_out, expert_ids, gate_probs, saved_gate, saved_up, master, moment_one, moment_two):
    tokens, D = grad_out.shape
    cap = tokens * 3 // 8
    slots, _, width = saved_gate.shape
    rows = master.shape[1]
    devices = NX * NZ * NC
    C, dc = CHUNKS, D // CHUNKS
    f32, bf16, i16 = jnp.float32, jnp.bfloat16, jnp.int16
    vm = pl.BlockSpec(memory_space=pltpu.VMEM)
    hbm = pl.BlockSpec(memory_space=pl.ANY)
    hrows = width // NC
    xrows = hrows // NX
    outs = pl.pallas_call(
        kernel,
        name="step",
        out_shape=(
            pltpu.VMEM((rows, D), f32),
            pltpu.VMEM((rows, D), f32),
            pltpu.VMEM((rows, D), f32),
            pltpu.VMEM((devices, rows, D + 128), i16),
        ),
        in_specs=[vm, vm] + [hbm] * 6,
        out_specs=(vm, vm, vm, vm),
        scratch_shapes=[
            pltpu.VMEM((C, tokens, dc), bf16),
            pltpu.VMEM((slots, width), bf16),
            pltpu.VMEM((slots, width), bf16),
            pltpu.VMEM((rows, D), f32),
            pltpu.VMEM((rows, D), f32),
            pltpu.VMEM((rows, D), f32),
            pltpu.VMEM((cap, tokens), bf16),
            pltpu.VMEM((cap, 128), f32),
            pltpu.VMEM((NC, hrows, slots), bf16),
            pltpu.VMEM((C, slots, dc), bf16),
            pltpu.VMEM((2, hrows, dc), f32),
            pltpu.VMEM((C, xrows, dc), f32),
            pltpu.VMEM((rows, D), f32),
            pltpu.VMEM((rows, 128), f32),
            pltpu.VMEM((rows, 128), f32),
            pltpu.VMEM((C, hrows, dc), f32),
            pltpu.VMEM((C, hrows, dc), f32),
            pltpu.VMEM((C, NX - 1, xrows, dc + 128), i16),
            pltpu.VMEM((C, NX - 1, xrows, dc + 128), i16),
            pltpu.VMEM((C, NZ - 1, rows, dc + 128), i16),
            pltpu.VMEM((C, NZ - 1, rows, dc + 128), i16),
            pltpu.VMEM((rows, D + 128), i16),
            pltpu.SemaphoreType.DMA((C + 5,)),
            pltpu.SemaphoreType.DMA((16, C)),
            pltpu.SemaphoreType.DMA((16, C)),
            pltpu.SemaphoreType.DMA((35,)),
            pltpu.SemaphoreType.DMA((35,)),
        ],
        compiler_params=pltpu.CompilerParams(
            collective_id=0, has_side_effects=True, vmem_limit_bytes=54 << 20),
    )(
        expert_ids.T, gate_probs.T, grad_out,
        saved_gate.reshape(slots, width), saved_up.reshape(slots, width),
        master.reshape(rows, D), moment_one.reshape(rows, D), moment_two.reshape(rows, D),
    )
    new, one, two, q = outs
    per = 8
    whole = pl.BlockSpec((rows, D), lambda i: (0, 0))
    full, new, one, two = pl.pallas_call(
        decode,
        name="decode",
        grid=(devices // per,),
        out_shape=(jax.ShapeDtypeStruct((devices * rows, D), f32),) + (jax.ShapeDtypeStruct((rows, D), f32),) * 3,
        in_specs=[vm, vm, vm, vm],
        out_specs=(pl.BlockSpec((per * rows, D), lambda i: (i, 0)), whole, whole, whole),
        compiler_params=pltpu.CompilerParams(vmem_limit_bytes=24 << 20),
    )(q, new, one, two)
    shape = master.shape
    return (new.reshape(shape), one.reshape(shape), two.reshape(shape), full.reshape(1, devices * rows, D))


def solution(mesh):
    return jax.shard_map(
        local,
        mesh=mesh,
        in_specs=(
            P(("dp", "expert"), None),
            P(("dp", "expert"), None),
            P(("dp", "expert"), None),
            P("dp", "expert", None),
            P("dp", "expert", None),
            P("expert", "dp", None),
            P("expert", "dp", None),
            P("expert", "dp", None),
        ),
        out_specs=(
            P("expert", "dp", None),
            P("expert", "dp", None),
            P("expert", "dp", None),
            P("expert", None, None),
        ),
        check_vma=False,
    )
```
